32 devices in a mesh: rep: 16 (over z, y, x), shard: 2 (over core).
Axes of the slice: x: 2, y: 2, z: 4, core: 2. Of those that a mesh axis runs over, the one named last changes fastest.
Arguments:
- tokens: bfloat16 [4096, 1024], P(('rep', 'shard')), may hold values from -6 to 6
- attn_gain: bfloat16 [1024], replicated, may hold values from 0.25 to 1.75
- query_weight: bfloat16 [1024, 2048], P(None, 'shard'), may hold values from -0.1875 to 0.1875
- key_weight: bfloat16 [1024, 1024], P(None, 'shard'), may hold values from -0.1875 to 0.1875
- value_weight: bfloat16 [1024, 1024], P(None, 'shard'), may hold values from -0.1875 to 0.1875
- query_gain: bfloat16 [128], replicated, may hold values from 0.5 to 8
- key_gain: bfloat16 [128], replicated, may hold values from 0.5 to 8
- out_weight: bfloat16 [2048, 1024], P('shard'), may hold values from -1 to 1
- mlp_gain: bfloat16 [1024], replicated, may hold values from 0.25 to 1.75
- gate_weight: bfloat16 [1024, 3072], P(None, 'shard'), may hold values from -0.1875 to 0.1875
- up_weight: bfloat16 [1024, 3072], P(None, 'shard'), may hold values from -0.1875 to 0.1875
- down_weight: bfloat16 [3072, 1024], P('shard'), may hold values from -0.109375 to 0.109375
- out_grad: bfloat16 [4096, 1024], P(('rep', 'shard')), may hold values from -6 to 6
Outputs:
- block_out: bfloat16 [4096, 1024], P(('rep', 'shard'))
- input_grad: float32 [4096, 1024], P(('rep', 'shard'))
- attn_gain_grad: float32 [1024], replicated
- query_weight_grad: float32 [1024, 2048], P(None, 'shard')
- key_weight_grad: float32 [1024, 1024], P(None, 'shard')
- value_weight_grad: float32 [1024, 1024], P(None, 'shard')
- query_gain_grad: float32 [128], replicated
- key_gain_grad: float32 [128], replicated
- out_weight_grad: float32 [2048, 1024], P('shard')
- mlp_gain_grad: float32 [1024], replicated
- gate_weight_grad: float32 [1024, 3072], P(None, 'shard')
- up_weight_grad: float32 [1024, 3072], P(None, 'shard')
- down_weight_grad: float32 [3072, 1024], P('shard')
The draws below stay inside these ranges and needn't reach their ends.
All inputs are finite; a program needn't handle non-finite values.
Results may differ from the reference program's by a relative error of at most 0.023.
The reference program's roundings to bfloat16 on the way count: a program that leaves them out, or rounds other values in their place, can miss the bound.
Values may be sent and summed in bfloat16 or wider, within the bound.
No kernel may reach another device: no remote copies, remote signals or barrier semaphores. Data moves between devices by JAX's collectives and lax.ppermute only.
A program may use at most 192 MiB of HBM per device.

```python
import math
import jax
import jax.numpy as jnp
from jax import lax

D = 1024
H = 16
KV = 8
HD = 128
FF = 3072
SEQ = 256
TOKENS = 4096
N_REP = 16


def gain_draw(key, salt):
    lower, upper = (0.7, 2.0)
    uniform_part = jax.random.uniform(jax.random.fold_in(key, salt), (HD,), jnp.float32)
    return jnp.exp(math.log(lower) + uniform_part * (math.log(upper) - math.log(lower)))


def draw_query_gain(key, part):
    return gain_draw(key, 11).astype(jnp.bfloat16)


def draw_key_gain(key, part):
    return gain_draw(key, 23).astype(jnp.bfloat16)


def shard_levels(own_key, dims, split, least, top_value):
    level, own = 1.0, jax.random.fold_in(own_key, 6)
    for position, blocks in split:
        steps = jnp.exp(jax.random.uniform(jax.random.fold_in(own, position), (blocks,), jnp.float32, least / len(split), top_value / len(split)))
        level = level * jnp.repeat(steps, dims[position] // blocks).reshape([-1 if axis == position else 1 for axis in range(len(dims))])
    return level


def normal_values(key, dims, scale, bound, pieces=(), kind=jnp.bfloat16):
    level = shard_levels(key, dims, pieces, -0.22, 0.18) if pieces else 1.0
    entries = jax.random.normal(key, dims, jnp.float32) * scale * level
    return jnp.minimum(jnp.maximum(entries, -bound), bound).astype(kind)


def setup_inputs(seed: int = 0) -> dict:
    key_of = jax.random.split(jax.random.key(seed), 14)
    tokens = normal_values(key_of[0], (TOKENS, D), 1.0, 6.0, ((0, 32),))
    attn_gain = jnp.clip(1.0 + 0.15 * jax.random.normal(key_of[1], (D,), jnp.float32), 0.25, 1.75).astype(jnp.bfloat16)
    query_weight = normal_values(key_of[2], (D, H * HD), D ** -0.5, 0.1875, ((1, 2),))
    key_weight = normal_values(key_of[3], (D, KV * HD), D ** -0.5, 0.1875, ((1, 2),))
    value_weight = normal_values(key_of[4], (D, KV * HD), D ** -0.5, 0.1875, ((1, 2),))
    query_gain = draw_query_gain(jax.random.fold_in(key_of[13], 71), 0)
    key_gain = draw_key_gain(jax.random.fold_in(key_of[13], 71), 0)
    out_weight = normal_values(key_of[7], (H * HD, D), (H * HD // 64) ** -0.5, 1.0, ((0, 2),))
    mlp_gain = jnp.clip(1.0 + 0.15 * jax.random.normal(key_of[8], (D,), jnp.float32), 0.25, 1.75).astype(jnp.bfloat16)
    gate_weight = normal_values(key_of[9], (D, FF), D ** -0.5, 0.1875, ((1, 2),))
    up_weight = normal_values(key_of[10], (D, FF), D ** -0.5, 0.1875, ((1, 2),))
    down_weight = normal_values(key_of[11], (FF, D), FF ** -0.5, 0.109375, ((0, 2),))
    out_grad = normal_values(key_of[12], (TOKENS, D), 1.0, 6.0, ((0, 32),))
    return {"tokens": tokens, "attn_gain": attn_gain, "query_weight": query_weight, "key_weight": key_weight, "value_weight": value_weight, "query_gain": query_gain, "key_gain": key_gain, "out_weight": out_weight, "mlp_gain": mlp_gain, "gate_weight": gate_weight, "up_weight": up_weight, "down_weight": down_weight, "out_grad": out_grad}


epsilon = 1e-06
rope_base = 1000000.0
masked_score = -1e+30

def rope_tables(positions, head_size):
    freq_index = jnp.arange(head_size // 2, dtype=jnp.float32)
    inverse = rope_base ** (-2.0 * freq_index / head_size)
    angles = positions.astype(jnp.float32)[:, None] * inverse[None, :]
    return (jnp.cos(angles)[:, None, :], jnp.sin(angles)[:, None, :])

def rotate(values, cos_table, sin_table):
    half_size = values.shape[-1] // 2
    first_half = values[..., :half_size]
    second_half = values[..., half_size:]
    return jnp.concatenate([first_half * cos_table - second_half * sin_table, second_half * cos_table + first_half * sin_table], axis=-1)

def rotate_back(grads, cos_table, sin_table):
    half_size = grads.shape[-1] // 2
    first_half = grads[..., :half_size]
    second_half = grads[..., half_size:]
    return jnp.concatenate([first_half * cos_table + second_half * sin_table, second_half * cos_table - first_half * sin_table], axis=-1)

def norm_forward(values, gain):
    scale_inv = lax.rsqrt(lax.optimization_barrier(jnp.mean(values * values, axis=-1, keepdims=True)) + epsilon)
    return (values * scale_inv * gain.astype(jnp.float32), scale_inv)

def norm_backward(grad_out, values, scale_inv, gain):
    lead_axes = tuple(range(values.ndim - 1))
    grad_gain = lax.optimization_barrier(jnp.sum(grad_out * values * scale_inv, axis=lead_axes))
    grad_unit = grad_out * gain.astype(jnp.float32)
    inner = lax.optimization_barrier(jnp.mean(grad_unit * values, axis=-1, keepdims=True))
    grad_values = scale_inv * (grad_unit - values * scale_inv * scale_inv * inner)
    return (grad_values, grad_gain)

def sequence_pass(token_rows, grad_rows, params):
    attn_gain, query_weight, key_weight, value_weight, query_gain, key_gain, out_weight, mlp_gain, gate_weight, up_weight, down_weight = params
    seq_rows = token_rows.shape[0]
    group_size = H // KV
    scale = HD ** (-0.5)
    positions = jnp.arange(seq_rows, dtype=jnp.int32)
    cos_table, sin_table = rope_tables(positions, HD)
    visible = (positions[None, :] <= positions[:, None])[None, None]
    residual_in = token_rows.astype(jnp.float32)
    normed_attn, attn_scale = norm_forward(residual_in, attn_gain)
    hidden_attn = normed_attn.astype(jnp.bfloat16)
    query_raw = jnp.dot(hidden_attn, query_weight, preferred_element_type=jnp.float32).reshape(seq_rows, H, HD)
    key_raw = jnp.dot(hidden_attn, key_weight, preferred_element_type=jnp.float32).reshape(seq_rows, KV, HD)
    value_rows = jnp.dot(hidden_attn, value_weight, preferred_element_type=jnp.float32).astype(jnp.bfloat16)
    value_grid = value_rows.reshape(seq_rows, KV, HD)
    query_normed, query_scale = norm_forward(query_raw, query_gain)
    key_normed, key_scale = norm_forward(key_raw, key_gain)
    query_rot = rotate(query_normed, cos_table, sin_table).astype(jnp.bfloat16).reshape(seq_rows, KV, group_size, HD)
    key_rot = rotate(key_normed, cos_table, sin_table).astype(jnp.bfloat16)
    scores = jnp.einsum('qkgd,tkd->kgqt', query_rot.astype(jnp.float32), key_rot.astype(jnp.float32)) * scale
    masked = jnp.where(visible, scores, masked_score)
    row_max = lax.optimization_barrier(jnp.max(masked, axis=-1))
    row_sum = lax.optimization_barrier(jnp.sum(jnp.where(visible, jnp.exp(masked - row_max[..., None]), 0.0), axis=-1))
    log_total = row_max + jnp.log(row_sum)
    weights_full = jnp.where(visible, jnp.exp(masked - log_total[..., None]), 0.0)
    weights = weights_full.astype(jnp.bfloat16)
    attn_grid = jnp.einsum('kgqt,tkd->qkgd', weights.astype(jnp.float32), value_grid.astype(jnp.float32))
    attn_rows = attn_grid.reshape(seq_rows, H * HD).astype(jnp.bfloat16)
    residual_mid = residual_in + jnp.dot(attn_rows, out_weight, preferred_element_type=jnp.float32)
    normed_mlp, mlp_scale = norm_forward(residual_mid, mlp_gain)
    hidden_mlp = normed_mlp.astype(jnp.bfloat16)
    gate_pre = jnp.dot(hidden_mlp, gate_weight, preferred_element_type=jnp.float32)
    up_pre = jnp.dot(hidden_mlp, up_weight, preferred_element_type=jnp.float32)
    gate_act = jax.nn.silu(gate_pre)
    product_rows = (gate_act * up_pre).astype(jnp.bfloat16)
    block_rows = residual_mid + jnp.dot(product_rows, down_weight, preferred_element_type=jnp.float32)
    block_out = block_rows.astype(jnp.bfloat16)
    down_terms = jnp.dot(product_rows.T, grad_rows, preferred_element_type=jnp.float32)
    grad_product = jnp.dot(grad_rows, down_weight.T, preferred_element_type=jnp.float32)
    sigmoid_gate = jax.nn.sigmoid(gate_pre)
    gate_slope = sigmoid_gate * (1.0 + gate_pre * (1.0 - sigmoid_gate))
    grad_gate = (grad_product * up_pre * gate_slope).astype(jnp.bfloat16)
    grad_up = (grad_product * gate_act).astype(jnp.bfloat16)
    gate_terms = jnp.dot(hidden_mlp.T, grad_gate, preferred_element_type=jnp.float32)
    up_terms = jnp.dot(hidden_mlp.T, grad_up, preferred_element_type=jnp.float32)
    grad_hidden_mlp = jnp.dot(grad_gate, gate_weight.T, preferred_element_type=jnp.float32) + jnp.dot(grad_up, up_weight.T, preferred_element_type=jnp.float32)
    grad_mid_norm, mlp_gain_terms = norm_backward(grad_hidden_mlp, residual_mid, mlp_scale, mlp_gain)
    grad_mid = grad_rows.astype(jnp.float32) + grad_mid_norm
    grad_mixed = grad_mid.astype(jnp.bfloat16)
    out_terms = jnp.dot(attn_rows.T, grad_mixed, preferred_element_type=jnp.float32)
    grad_attn = jnp.dot(grad_mixed, out_weight.T, preferred_element_type=jnp.float32).astype(jnp.bfloat16)
    grad_attn_grid = grad_attn.reshape(seq_rows, KV, group_size, HD)
    delta = jnp.transpose(lax.optimization_barrier(jnp.sum(grad_attn_grid.astype(jnp.float32) * attn_rows.reshape(seq_rows, KV, group_size, HD).astype(jnp.float32), axis=-1)), (1, 2, 0))
    grad_weights = jnp.einsum('qkgd,tkd->kgqt', grad_attn_grid.astype(jnp.float32), value_grid.astype(jnp.float32))
    grad_scores = (weights_full * (grad_weights - delta[..., None]) * scale).astype(jnp.bfloat16)
    grad_query_rot = jnp.einsum('kgqt,tkd->qkgd', grad_scores.astype(jnp.float32), key_rot.astype(jnp.float32)).reshape(seq_rows, H, HD)
    key_rot_grad = jnp.einsum('kgqt,qkgd->tkd', grad_scores.astype(jnp.float32), query_rot.astype(jnp.float32))
    value_grad = jnp.einsum('kgqt,qkgd->tkd', weights.astype(jnp.float32), grad_attn_grid.astype(jnp.float32))
    grad_query_raw, query_gain_terms = norm_backward(rotate_back(grad_query_rot, cos_table, sin_table), query_raw, query_scale, query_gain)
    grad_key_raw, key_gain_terms = norm_backward(rotate_back(key_rot_grad, cos_table, sin_table), key_raw, key_scale, key_gain)
    grad_query = grad_query_raw.reshape(seq_rows, H * HD).astype(jnp.bfloat16)
    grad_key = grad_key_raw.reshape(seq_rows, KV * HD).astype(jnp.bfloat16)
    grad_value = value_grad.reshape(seq_rows, KV * HD).astype(jnp.bfloat16)
    query_terms = jnp.dot(hidden_attn.T, grad_query, preferred_element_type=jnp.float32)
    key_terms = jnp.dot(hidden_attn.T, grad_key, preferred_element_type=jnp.float32)
    value_terms = jnp.dot(hidden_attn.T, grad_value, preferred_element_type=jnp.float32)
    grad_hidden_attn = jnp.dot(grad_query, query_weight.T, preferred_element_type=jnp.float32) + jnp.dot(grad_key, key_weight.T, preferred_element_type=jnp.float32) + jnp.dot(grad_value, value_weight.T, preferred_element_type=jnp.float32)
    grad_in_norm, attn_gain_terms = norm_backward(grad_hidden_attn, residual_in, attn_scale, attn_gain)
    input_grad = grad_mid + grad_in_norm
    terms = (attn_gain_terms, query_terms, key_terms, value_terms, query_gain_terms, key_gain_terms, out_terms, mlp_gain_terms, gate_terms, up_terms, down_terms)
    return (block_out, input_grad, terms)

def reference(tokens, attn_gain, query_weight, key_weight, value_weight, query_gain, key_gain, out_weight, mlp_gain, gate_weight, up_weight, down_weight, out_grad):
    params = (attn_gain, query_weight, key_weight, value_weight, query_gain, key_gain, out_weight, mlp_gain, gate_weight, up_weight, down_weight)
    token_blocks = tokens.reshape(N_REP, SEQ, D)
    grad_blocks = out_grad.reshape(N_REP, SEQ, D)
    starting = tuple((jnp.zeros(param.shape, jnp.float32) for param in params))

    def step_fn(totals, inputs):
        block_out, input_grad, terms = sequence_pass(inputs[0], inputs[1], params)
        return (tuple((total + term for total, term in zip(totals, terms))), (block_out, input_grad))
    totals, (outputs, input_grads) = lax.scan(step_fn, starting, (token_blocks, grad_blocks))
    return (outputs.reshape(TOKENS, D), input_grads.reshape(TOKENS, D), totals[0], totals[1], totals[2], totals[3], totals[4], totals[5], totals[6], totals[7], totals[8], totals[9], totals[10])
```

```python
import jax
import jax.numpy as jnp
from jax import lax
from jax.sharding import PartitionSpec as P

epsilon = 1e-06
rope_base = 1000000.0
masked_score = -1e30


def rope_tables(positions, head_size):
    freq_index = jnp.arange(head_size // 2, dtype=jnp.float32)
    inverse = rope_base ** (-2.0 * freq_index / head_size)
    angles = positions.astype(jnp.float32)[:, None] * inverse[None, :]
    return (jnp.cos(angles)[:, None, :], jnp.sin(angles)[:, None, :])


def rotate(values, cos_table, sin_table):
    half_size = values.shape[-1] // 2
    first_half = values[..., :half_size]
    second_half = values[..., half_size:]
    return jnp.concatenate(
        [
            first_half * cos_table - second_half * sin_table,
            second_half * cos_table + first_half * sin_table,
        ],
        axis=-1,
    )


def rotate_back(grads, cos_table, sin_table):
    half_size = grads.shape[-1] // 2
    first_half = grads[..., :half_size]
    second_half = grads[..., half_size:]
    return jnp.concatenate(
        [
            first_half * cos_table + second_half * sin_table,
            second_half * cos_table - first_half * sin_table,
        ],
        axis=-1,
    )


def norm_forward(values, gain):
    scale_inv = lax.rsqrt(jnp.mean(values * values, axis=-1, keepdims=True) + epsilon)
    return (values * scale_inv * gain.astype(jnp.float32), scale_inv)


def norm_backward(grad_out, values, scale_inv, gain):
    lead_axes = tuple(range(values.ndim - 1))
    grad_gain = jnp.sum(grad_out * values * scale_inv, axis=lead_axes)
    grad_unit = grad_out * gain.astype(jnp.float32)
    inner = jnp.mean(grad_unit * values, axis=-1, keepdims=True)
    grad_values = scale_inv * (grad_unit - values * scale_inv * scale_inv * inner)
    return (grad_values, grad_gain)


def outer_terms(left, right):
    return lax.dot_general(
        left, right, (((0,), (0,)), ((), ())), preferred_element_type=jnp.float32
    )


def times_transposed(left, right):
    return lax.dot_general(
        left, right, (((1,), (1,)), ((), ())), preferred_element_type=jnp.float32
    )


class Links:
    def __init__(self, n_rep, n_shard):
        self.n_rep = n_rep
        self.n_shard = n_shard
        self.quad = 4
        self.n_line = n_rep // self.quad
        self.place = lax.axis_index("rep") % self.quad
        self.line = lax.axis_index("rep") // self.quad

    def swap(self, value, bits):
        return lax.ppermute(value, "rep", [(i, i ^ bits) for i in range(self.n_rep)])

    def hop(self, value, direction, first, last):
        pairs = [
            (z * self.quad + q, (z + direction) * self.quad + q)
            for z in range(first, last + 1)
            for q in range(self.quad)
        ]
        return lax.ppermute(value, "rep", pairs)

    def partner(self, value):
        return lax.ppermute(value, "shard", [(0, 1), (1, 0)])

    def row_positions(self, own_rows):
        if self.n_shard == 2:
            core = lax.axis_index("shard")
            span = jnp.arange(own_rows, dtype=jnp.int32)
            return jnp.concatenate([core * own_rows + span, (1 - core) * own_rows + span])
        return jnp.arange(own_rows * self.n_shard, dtype=jnp.int32)

    def gather(self, value, axis=0):
        if self.n_shard == 2:
            return jnp.concatenate([value, self.partner(value)], axis=axis)
        return lax.all_gather(value, "shard", axis=axis, tiled=True)

    def scatter(self, partial):
        if self.n_shard == 2:
            own_rows = partial.shape[0] // 2
            other = self.partner(partial[own_rows:].astype(jnp.bfloat16))
            return partial[:own_rows] + other.astype(jnp.float32)
        return lax.psum_scatter(
            partial.astype(jnp.bfloat16), "shard", scatter_dimension=0, tiled=True
        ).astype(jnp.float32)

    def total(self, vector):
        bit = 1
        while bit < self.n_shard:
            vector = vector + lax.ppermute(
                vector, "shard", [(i, i ^ bit) for i in range(self.n_shard)]
            )
            bit *= 2
        bit = 1
        while bit < self.n_rep:
            vector = vector + self.swap(vector, bit)
            bit *= 2
        return vector

    def quad_rows(self, own):
        stacked = jnp.stack([own] + [self.swap(own, k) for k in range(1, self.quad)])
        rows = self.gather(stacked, axis=1)
        return rows.reshape(-1, own.shape[-1])

    def quad_columns(self, parts):
        def pick(place):
            cut = [
                lax.dynamic_slice_in_dim(part, place * (part.shape[1] // self.quad), part.shape[1] // self.quad, 1)
                for part in parts
            ]
            return cut[0] if len(cut) == 1 else jnp.concatenate(cut, axis=1)

        pieces = [pick(self.place)]
        for k in range(1, self.quad):
            pieces.append(self.swap(pick(self.place ^ k), k))
        return jnp.concatenate(pieces, axis=0)

    def line_scatter(self, terms):
        n = self.n_line
        chunks = terms.reshape(n, terms.shape[0] // n, terms.shape[1])

        def own(index):
            index = jnp.clip(index, 0, n - 1)
            return lax.dynamic_index_in_dim(chunks, index, 0, keepdims=False).astype(jnp.float32)

        up, down = None, None
        for s in range(1, n):
            send = own(n - s + self.line)
            if up is not None:
                send = send + up.astype(jnp.float32)
            up = self.hop(send.astype(jnp.bfloat16), 1, 0, s - 1)
            send = own(s - n + self.line)
            if down is not None:
                send = send + down.astype(jnp.float32)
            down = self.hop(send.astype(jnp.bfloat16), -1, n - s, n - 1)
        total = own(self.line)
        if n > 1:
            total = total + up.astype(jnp.float32) + down.astype(jnp.float32)
        return total.astype(jnp.bfloat16)

    def line_gather(self, piece):
        n = self.n_line
        up, down = [piece], [piece]
        for s in range(1, n):
            up.append(self.hop(up[-1], 1, s - 1, n - 2))
            down.append(self.hop(down[-1], -1, 1, n - s))
        rows = piece.shape[0]
        out = jnp.zeros((n * rows, piece.shape[1]), piece.dtype)
        for s in range(n):
            got = piece if s == 0 else jnp.where(self.line >= s, up[s], down[n - s])
            where = jnp.remainder(self.line - s, n)
            out = lax.dynamic_update_slice_in_dim(out, got, where * rows, 0)
        return out

    def quad_gather(self, quarter):
        half = quarter.shape[0] // 2
        across_x = self.swap(quarter, 1)
        across_y = self.swap(quarter, 2)
        upper = self.swap(across_y[:half], 1)
        lower = self.swap(across_x[half:], 2)
        return [(0, 0, quarter), (1, 0, across_x), (2, 0, across_y), (3, 0, upper), (3, half, lower)]

    def reduce(self, terms):
        return self.quad_gather(self.line_gather(self.line_scatter(terms.astype(jnp.bfloat16))))

    def place_columns(self, pieces, widths, rows):
        outs = []
        offset = 0
        for width in widths:
            out = jnp.zeros((rows, self.quad * width), jnp.float32)
            for bits, first, piece in pieces:
                cut = piece[:, offset : offset + width].astype(jnp.float32)
                out = lax.dynamic_update_slice(out, cut, (first, (self.place ^ bits) * width))
            outs.append(out)
            offset += width
        return outs

    def place_rows(self, pieces, height, width):
        out = jnp.zeros((self.quad * height, width), jnp.float32)
        for bits, first, piece in pieces:
            out = lax.dynamic_update_slice(
                out, piece.astype(jnp.float32), ((self.place ^ bits) * height + first, 0)
            )
        return out


def body_on(n_rep, n_shard):
    def body(
        tokens,
        attn_gain,
        query_weight,
        key_weight,
        value_weight,
        query_gain,
        key_gain,
        out_weight,
        mlp_gain,
        gate_weight,
        up_weight,
        down_weight,
        out_grad,
    ):
        links = Links(n_rep, n_shard)
        quad = links.quad
        head_size = query_gain.shape[0]
        query_heads = query_weight.shape[1] // head_size
        kv_heads = key_weight.shape[1] // head_size
        group_size = query_heads // kv_heads
        scale = head_size ** (-0.5)
        width = tokens.shape[1]
        residual_in = tokens.astype(jnp.float32)
        normed_attn, attn_scale = norm_forward(residual_in, attn_gain)
        hidden_attn = normed_attn.astype(jnp.bfloat16)
        attn_inputs = links.gather(hidden_attn)
        cotangent_all = links.gather(out_grad)
        seq_rows = attn_inputs.shape[0]
        positions = links.row_positions(tokens.shape[0])
        cos_table, sin_table = rope_tables(positions, head_size)
        query_raw = jnp.dot(attn_inputs, query_weight, preferred_element_type=jnp.float32).reshape(
            seq_rows, query_heads, head_size
        )
        key_raw = jnp.dot(attn_inputs, key_weight, preferred_element_type=jnp.float32).reshape(
            seq_rows, kv_heads, head_size
        )
        value_rows = jnp.dot(attn_inputs, value_weight, preferred_element_type=jnp.float32).astype(
            jnp.bfloat16
        )
        value_grid = value_rows.reshape(seq_rows, kv_heads, head_size)
        query_normed, query_scale = norm_forward(query_raw, query_gain)
        key_normed, key_scale = norm_forward(key_raw, key_gain)
        query_rot = (
            rotate(query_normed, cos_table, sin_table)
            .astype(jnp.bfloat16)
            .reshape(seq_rows, kv_heads, group_size, head_size)
        )
        key_rot = rotate(key_normed, cos_table, sin_table).astype(jnp.bfloat16)

        visible = (positions[None, :] <= positions[:, None])[None, None]
        scores = (
            jnp.einsum("qkgd,tkd->kgqt", query_rot, key_rot, preferred_element_type=jnp.float32)
            * scale
        )
        masked = jnp.where(visible, scores, masked_score)
        row_max = jnp.max(masked, axis=-1)
        row_sum = jnp.sum(jnp.where(visible, jnp.exp(masked - row_max[..., None]), 0.0), axis=-1)
        log_total = row_max + jnp.log(row_sum)
        weights_full = jnp.where(visible, jnp.exp(masked - log_total[..., None]), 0.0)
        weights = weights_full.astype(jnp.bfloat16)
        attn_rows = (
            jnp.einsum("kgqt,tkd->qkgd", weights, value_grid, preferred_element_type=jnp.float32)
            .reshape(seq_rows, query_heads * head_size)
            .astype(jnp.bfloat16)
        )
        attn_out = links.scatter(
            jnp.dot(attn_rows, out_weight, preferred_element_type=jnp.float32)
        )
        residual_mid = residual_in + attn_out
        normed_mlp, mlp_scale = norm_forward(residual_mid, mlp_gain)
        hidden_mlp = normed_mlp.astype(jnp.bfloat16)
        mlp_inputs = links.gather(hidden_mlp)
        gate_pre = jnp.dot(mlp_inputs, gate_weight, preferred_element_type=jnp.float32)
        up_pre = jnp.dot(mlp_inputs, up_weight, preferred_element_type=jnp.float32)
        gate_act = jax.nn.silu(gate_pre)
        product_rows = (gate_act * up_pre).astype(jnp.bfloat16)
        down_out = links.scatter(
            jnp.dot(product_rows, down_weight, preferred_element_type=jnp.float32)
        )
        block_out = (residual_mid + down_out).astype(jnp.bfloat16)

        down_quarter = outer_terms(links.quad_columns([product_rows]), links.quad_rows(out_grad))
        down_pieces = links.reduce(down_quarter)

        grad_product = times_transposed(cotangent_all, down_weight)
        sigmoid_gate = jax.nn.sigmoid(gate_pre)
        gate_slope = sigmoid_gate * (1.0 + gate_pre * (1.0 - sigmoid_gate))
        grad_gate = (grad_product * up_pre * gate_slope).astype(jnp.bfloat16)
        grad_up = (grad_product * gate_act).astype(jnp.bfloat16)

        gate_up_quarter = outer_terms(
            links.quad_rows(hidden_mlp), links.quad_columns([grad_gate, grad_up])
        )
        gate_up_pieces = links.reduce(gate_up_quarter)

        grad_hidden_mlp = links.scatter(
            times_transposed(grad_gate, gate_weight) + times_transposed(grad_up, up_weight)
        )
        grad_mid_norm, mlp_gain_terms = norm_backward(
            grad_hidden_mlp, residual_mid, mlp_scale, mlp_gain
        )
        grad_mid = out_grad.astype(jnp.float32) + grad_mid_norm
        grad_mixed = grad_mid.astype(jnp.bfloat16)
        mixed_all = links.gather(grad_mixed)

        out_quarter = outer_terms(links.quad_columns([attn_rows]), links.quad_rows(grad_mixed))
        out_pieces = links.reduce(out_quarter)

        grad_attn = (
            times_transposed(mixed_all, out_weight)
            .astype(jnp.bfloat16)
            .reshape(seq_rows, kv_heads, group_size, head_size)
        )
        attn_grid = attn_rows.reshape(seq_rows, kv_heads, group_size, head_size)
        delta = jnp.transpose(
            jnp.sum(grad_attn.astype(jnp.float32) * attn_grid.astype(jnp.float32), axis=-1),
            (1, 2, 0),
        )
        grad_weights = jnp.einsum(
            "qkgd,tkd->kgqt", grad_attn, value_grid, preferred_element_type=jnp.float32
        )
        grad_scores = (weights_full * (grad_weights - delta[..., None]) * scale).astype(
            jnp.bfloat16
        )
        grad_query_rot = jnp.einsum(
            "kgqt,tkd->qkgd", grad_scores, key_rot, preferred_element_type=jnp.float32
        ).reshape(seq_rows, query_heads, head_size)
        key_accum = jnp.einsum(
            "kgqt,qkgd->tkd", grad_scores, query_rot, preferred_element_type=jnp.float32
        )
        value_accum = jnp.einsum(
            "kgqt,qkgd->tkd", weights, grad_attn, preferred_element_type=jnp.float32
        )
        grad_query_raw, query_gain_terms = norm_backward(
            rotate_back(grad_query_rot, cos_table, sin_table), query_raw, query_scale, query_gain
        )
        grad_key_raw, key_gain_terms = norm_backward(
            rotate_back(key_accum, cos_table, sin_table), key_raw, key_scale, key_gain
        )
        grad_query = grad_query_raw.reshape(seq_rows, query_heads * head_size).astype(jnp.bfloat16)
        grad_key = grad_key_raw.reshape(seq_rows, kv_heads * head_size).astype(jnp.bfloat16)
        grad_value = value_accum.reshape(seq_rows, kv_heads * head_size).astype(jnp.bfloat16)

        qkv_quarter = outer_terms(
            links.quad_rows(hidden_attn), links.quad_columns([grad_query, grad_key, grad_value])
        )
        qkv_pieces = links.reduce(qkv_quarter)

        partial_sum = times_transposed(grad_query, query_weight)
        partial_sum = partial_sum + times_transposed(grad_key, key_weight)
        grad_hidden_attn = links.scatter(partial_sum + times_transposed(grad_value, value_weight))
        grad_in_norm, attn_gain_terms = norm_backward(
            grad_hidden_attn, residual_in, attn_scale, attn_gain
        )
        input_grad = grad_mid + grad_in_norm

        gains = links.total(
            jnp.concatenate(
                [
                    attn_gain_terms,
                    mlp_gain_terms,
                    query_gain_terms,
                    key_gain_terms,
                ]
            )
        )
        attn_gain_grad = gains[:width]
        mlp_gain_grad = gains[width : 2 * width]
        query_gain_grad = gains[2 * width : 2 * width + head_size]
        key_gain_grad = gains[2 * width + head_size :]

        down_grad = links.place_rows(down_pieces, product_rows.shape[1] // quad, width)
        gate_grad, up_grad = links.place_columns(
            gate_up_pieces, [gate_weight.shape[1] // quad, up_weight.shape[1] // quad], width
        )
        out_weight_grad = links.place_rows(out_pieces, attn_rows.shape[1] // quad, width)
        query_grad, key_grad, value_grad = links.place_columns(
            qkv_pieces,
            [query_weight.shape[1] // quad, key_weight.shape[1] // quad, value_weight.shape[1] // quad],
            width,
        )
        return (
            block_out,
            input_grad,
            attn_gain_grad,
            query_grad,
            key_grad,
            value_grad,
            query_gain_grad,
            key_gain_grad,
            out_weight_grad,
            mlp_gain_grad,
            gate_grad,
            up_grad,
            down_grad,
        )

    return body


def solution(mesh):
    placed = (
        P(("rep", "shard"), None),
        P(),
        P(None, "shard"),
        P(None, "shard"),
        P(None, "shard"),
        P(),
        P(),
        P("shard", None),
        P(),
        P(None, "shard"),
        P(None, "shard"),
        P("shard", None),
        P(("rep", "shard"), None),
    )
    return jax.shard_map(
        body_on(mesh.shape["rep"], mesh.shape["shard"]),
        mesh=mesh,
        in_specs=placed,
        out_specs=(
            P(("rep", "shard"), None),
            P(("rep", "shard"), None),
            P(),
            P(None, "shard"),
            P(None, "shard"),
            P(None, "shard"),
            P(),
            P(),
            P("shard", None),
            P(),
            P(None, "shard"),
            P(None, "shard"),
            P("shard", None),
        ),
        check_vma=False,
    )
```
